32 devices in a mesh: ens: 2 (over x), lat: 16 (over z, y, core).
Axes of the slice: x: 2, y: 2, z: 4, core: 2. Of those that a mesh axis runs over, the one named last changes fastest.
Arguments:
- members: float32 [80, 2, 64, 640], P('lat', 'ens'), may hold values from -24 to 24
- truth: float32 [4, 80, 64, 640], P(None, 'lat'), may hold values from -32 to 32
- target_time: int32 [80], P('lat'), may hold values from 0 to 3
- row_taps: int32 [1, 80, 5], P(None, 'lat'), may hold values from 0 to 79, as said below
- filters: float32 [1, 80, 5, 9, 5], P(None, 'lat'), may hold values from -1.2 to 1.2
- mixing: float32 [1, 64, 9, 64], replicated, may hold values from -0.25 to 0.25
Outputs:
- score_grad: float32 [80, 2, 64, 640], P('lat', 'ens')
- loss_value: float32 [1], replicated
The draws below stay inside these ranges and needn't reach their ends.
Inputs may be any that keep to these rules, and one draw needn't show every extreme that they name: row_taps[l, i, t] lies within 4 rows of i; in every layer some row lists a row exactly 4 below it and some row one exactly 4 above it. `target_time`: selects one of the stored target fields for each latitude row.
All inputs are finite; a program needn't handle non-finite values.
Results may differ from the reference program's by a relative error of at most 0.0003.
Values sent between devices are 32-bit elements; how exact they have to be, the bound alone decides.
No kernel may reach another device: no remote copies, remote signals or barrier semaphores. Data moves between devices by JAX's collectives and lax.ppermute only.
A program may use at most 64 MiB of HBM per device.

```python
import math
import jax
import jax.numpy as jnp
from jax import lax

C = 64
NLON = 640
K = 9
TAPS = 5
LW = 5
REACH = 4
LAYERS = 1
TIMES = 4
ENS = 2
NLAT = 80


def draw_row_taps(key, part):
    key_offsets = jax.random.fold_in(key, 11)
    key_chosen = jax.random.fold_in(key, 12)
    row_ids = jnp.arange(NLAT, dtype=jnp.int32)[None, :, None]
    tap_slots = jnp.arange(TAPS, dtype=jnp.int32)[None, None, :]
    offsets = jax.random.randint(key_offsets, (LAYERS, NLAT, TAPS), -REACH, REACH + 1, dtype=jnp.int32)
    chosen = jax.random.randint(key_chosen, (LAYERS, 2), REACH, NLAT - REACH, dtype=jnp.int32)
    upper_mask = (row_ids == chosen[:, 0][:, None, None]) & (tap_slots == 0)
    lower_mask = (row_ids == chosen[:, 1][:, None, None]) & (tap_slots == 1)
    offsets = jnp.where(upper_mask, -REACH, offsets)
    offsets = jnp.where(lower_mask, REACH, offsets)
    return jnp.clip(row_ids + offsets, 0, NLAT - 1).astype(jnp.int32)


def draw_members(key, part):
    key_noise = jax.random.fold_in(key, 21)
    fraction = jnp.arange(ENS, dtype=jnp.float32)
    scales = 6.0 ** fraction
    noise = jnp.clip(jax.random.normal(key_noise, (NLAT, ENS, C, NLON), jnp.float32), -4.0, 4.0)
    return (noise * scales[None, :, None, None]).astype(jnp.float32)


def draw_truth(key, part):
    key_noise = jax.random.fold_in(key, 31)
    fraction = jnp.arange(NLON, dtype=jnp.float32) / (NLON - 1.0)
    scales = 8.0 ** fraction
    noise = jnp.clip(jax.random.normal(key_noise, (TIMES, NLAT, C, NLON), jnp.float32), -4.0, 4.0)
    return (noise * scales[None, None, None, :]).astype(jnp.float32)


def touch_ends(array, own_key, low, largest):
    longest = array.shape.index(max(array.shape))
    spots = []
    for shift in (0, 1):
        where = [jax.random.randint(jax.random.fold_in(own_key, axis), (), 0, length) for axis, length in enumerate(array.shape)]
        where[longest] = (where[longest] + shift) % array.shape[longest]
        spots.append(tuple(where))
    return array.at[spots[0]].set(low).at[spots[1]].set(largest)


def level_of(rng, shape, split, smallest, largest):
    def one(axis_at, blocks):
        draws = jax.random.uniform(jax.random.fold_in(jax.random.fold_in(rng, 6), axis_at), (blocks,), jnp.float32, smallest / len(split), largest / len(split))
        return jnp.repeat(jnp.exp(draws), shape[axis_at] // blocks).reshape((-1,) + (1,) * (len(shape) - axis_at - 1))

    gain = one(*split[0])
    for cut in split[1:]:
        gain = gain * one(*cut)
    return gain


def bell_draw(own_key, extent, scale, limit, shards=(), kind=jnp.bfloat16):
    factor_of = level_of(own_key, extent, shards, -0.22, 0.18) if shards else 1.0
    array = jax.random.normal(own_key, extent, jnp.float32) * scale * factor_of
    return jnp.minimum(jnp.maximum(array, -limit), limit).astype(kind)


def setup_inputs(seed: int = 0) -> dict:
    key_list = jax.random.split(jax.random.key(seed), 7)
    members = draw_members(jax.random.fold_in(key_list[6], 71), 0)
    truth = draw_truth(jax.random.fold_in(key_list[6], 71), 0)
    target_time = touch_ends(jax.random.randint(key_list[2], (NLAT,), 0, TIMES), jax.random.fold_in(key_list[2], 1), 0, TIMES - 1).astype(jnp.int32)
    row_taps = draw_row_taps(jax.random.fold_in(key_list[6], 71), 0)
    filters = bell_draw(key_list[4], (LAYERS, NLAT, TAPS, K, LW), 0.2, 1.2, ((1, 16),), jnp.float32)
    mixing = bell_draw(key_list[5], (LAYERS, C, K, C), (K * C) ** -0.5, 0.25, (), jnp.float32)
    return {"members": members, "truth": truth, "target_time": target_time, "row_taps": row_taps, "filters": filters, "mixing": mixing}


def reference(members, truth, target_time, row_taps, filters, mixing):
    highest = lax.Precision.HIGHEST
    half_width = LW // 2
    fields = members
    for layer_number in range(LAYERS):
        weight = mixing[layer_number]

        def one_row(row_inputs):
            tap_rows, row_filter = row_inputs
            picked = jnp.take(fields, tap_rows.astype(jnp.int32), axis=0)
            shifted = jnp.stack([jnp.roll(picked, half_width - lon_lag, axis=-1) for lon_lag in range(LW)], axis=1)
            basis_out = jnp.einsum('tkd,tdmcj->kmcj', row_filter.astype(jnp.float32), shifted.astype(jnp.float32), precision=highest)
            return jnp.einsum('okc,kmcj->moj', weight.astype(jnp.float32), basis_out, precision=highest)
        mixed_out = lax.map(one_row, (row_taps[layer_number], filters[layer_number]))
        fields = fields + jax.nn.gelu(mixed_out, approximate=True)
    row_index = jnp.arange(NLAT, dtype=jnp.int32)
    target = truth[target_time.astype(jnp.int32), row_index]
    latitude = (jnp.arange(NLAT, dtype=jnp.float32) + 0.5) * (math.pi / NLAT) - 0.5 * math.pi
    cosine = jnp.cos(latitude)
    area = cosine / jnp.mean(cosine)
    to_truth = fields - target[:, None]
    skill_dist = jnp.sqrt(lax.optimization_barrier(jnp.mean(to_truth * to_truth, axis=2)) + 1.0)

    def pair_terms(member):
        gap_field = member[:, None] - fields
        distance = jnp.sqrt(lax.optimization_barrier(jnp.mean(gap_field * gap_field, axis=2)) + 1.0)
        return (lax.optimization_barrier(jnp.sum(gap_field / distance[:, :, None], axis=1)), lax.optimization_barrier(jnp.sum(distance, axis=1)))
    pull_sum, spread = lax.map(pair_terms, jnp.moveaxis(fields, 1, 0))
    score_grad = area[:, None, None, None] * (to_truth / skill_dist[:, :, None] - jnp.moveaxis(pull_sum, 0, 1) / ENS)
    per_cell = lax.optimization_barrier(jnp.sum(skill_dist, axis=1)) / ENS - lax.optimization_barrier(jnp.sum(spread, axis=0)) / (2.0 * ENS * ENS)
    loss_value = jnp.sum(area[:, None] * per_cell) / (NLAT * NLON)
    return (score_grad, jnp.reshape(loss_value, (1,)))
```

```python
import functools
import math

import jax
import jax.numpy as jnp
import numpy as np
from jax import lax
from jax.experimental import pallas as pl
from jax.experimental.pallas import tpu as pltpu
from jax.sharding import PartitionSpec as P

REACH = 4
LANES = 128
GROUP = 8
MIB = 1 << 20

VMEM = pl.BlockSpec(memory_space=pltpu.VMEM)
SMEM = pl.BlockSpec(memory_space=pltpu.SMEM)
ANY = pl.BlockSpec(memory_space=pl.ANY)


def round_up(value, unit):
    return -(-value // unit) * unit


def shift_left(cells, amount):
    width = cells.shape[-1]
    amount %= width
    return cells if amount == 0 else pltpu.roll(cells, width - amount, axis=cells.ndim - 1)


def pack_rows(ref, at, cells, width):
    groups = cells.shape[0] // GROUP
    lane = lax.broadcasted_iota(jnp.int32, (GROUP, LANES), 1)
    held = None
    for group in range(groups):
        part = cells[group * GROUP : (group + 1) * GROUP]
        first, last = group * width, (group + 1) * width
        offset = first % LANES
        tiles = -(-(offset + width) // LANES)
        pad = tiles * LANES - part.shape[1]
        if pad > 0:
            part = jnp.concatenate([part, jnp.zeros((GROUP, pad), part.dtype)], axis=1)
        if offset:
            part = pltpu.roll(part, offset, axis=1)
        base = first // LANES
        for tile in range(tiles):
            value = part[:, tile * LANES : (tile + 1) * LANES]
            if tile == 0 and offset:
                value = jnp.where(lane < offset, held, value)
            if (base + tile + 1) * LANES <= last or group == groups - 1:
                ref[at + (slice(None), pl.ds((base + tile) * LANES, LANES))] = value
            else:
                held = value


def unpack_rows(ref, at, groups, width, wide):
    parts = []
    limit = ref.shape[-1]
    for group in range(groups):
        first = group * width
        offset = first % LANES
        base = first - offset
        take = min(wide + (LANES if offset else 0), limit - base)
        part = ref[at + (slice(None), pl.ds(base, take))]
        if take < wide:
            part = jnp.concatenate([part, jnp.zeros((GROUP, wide - take), part.dtype)], axis=1)
        if offset:
            part = shift_left(part, offset)
        parts.append(part[:, :wide])
    return jnp.concatenate(parts, axis=0)


def gelu(v):
    return 0.5 * v * (1.0 + jnp.tanh(math.sqrt(2.0 / math.pi) * (v + 0.044715 * (v * v * v))))


def prepare_kernel(sizes, members, own_w, near_own, far_own, oth, far_oth):
    band, n, w, reach2, wide = sizes
    ens = lax.axis_index("ens")
    odd = lax.rem(lax.axis_index("lat"), 2)
    total = members.shape[3]
    kept = w + 2 * reach2

    def one_row(r, _):
        row = members[r, 0]

        def window(owner):
            start = lax.rem(owner * w - reach2 + total, total)
            return pltpu.roll(row, lax.rem(total - start, total), axis=1)[:, :wide]

        own = window(ens)
        own_w[r] = own

        near_at = r - (1 - odd)
        far_at = r - odd
        keep_near = jnp.logical_and(near_at >= 0, near_at < REACH)
        keep_far = jnp.logical_and(far_at >= 0, far_at < REACH)

        @pl.when(keep_near)
        def _():
            pack_rows(near_own, (near_at,), own, kept)

        @pl.when(keep_far)
        def _():
            pack_rows(far_own, (far_at,), own, kept)

        for step in range(1, n):
            cells = window(lax.rem(ens + step, n))
            pack_rows(oth, (step - 1, r), cells, kept)

            @pl.when(keep_far)
            def _():
                far_oth[step - 1, far_at] = oth[step - 1, r]

        return 0

    lax.fori_loop(0, band, one_row, 0)


def weights_kernel(sizes, times, filters, mix, truth, weights, target, held, sems):
    band, taps, lags, kinds, w, wide = sizes
    ens = lax.axis_index("ens")
    total = truth.shape[3]
    copies = [
        pltpu.make_async_copy(truth.at[times[r], r], held.at[r], sems.at[r]) for r in range(band)
    ]
    for copy in copies:
        copy.start()
    c = mix.shape[1]
    half = lax.broadcasted_iota(jnp.int32, (c, 2 * c), 1) < c

    def one_row(r, _):
        for d in range(lags):
            rows = pl.ds(d * c, c)
            before = None
            for t in range(taps):
                acc = filters[r * taps + t, d] * mix[0]
                for k in range(1, kinds):
                    acc = acc + filters[r * taps + t, k * lags + d] * mix[k]
                high = acc.astype(jnp.bfloat16).astype(jnp.float32)
                low = acc - high
                weights[r, rows, pl.ds(t * 2 * c, 2 * c)] = jnp.where(half, high, low).astype(
                    jnp.bfloat16
                )
                if t % 2:
                    pair = jnp.where(half, before, high)
                elif t == taps - 1:
                    pair = jnp.where(half, high, 0.0)
                if t % 2 or t == taps - 1:
                    weights[r, rows, pl.ds((taps + t // 2) * 2 * c, 2 * c)] = pair.astype(jnp.bfloat16)
                before = high
        return 0

    lax.fori_loop(0, band, one_row, 0)
    for copy in copies:
        copy.wait()

    def cut(r, _):
        turn = lax.rem(total - ens * w, total)
        target[r] = pltpu.roll(held[r], turn, axis=1)[:, :wide]
        return 0

    lax.fori_loop(0, band, cut, 0)


def store_split(split, q, cells):
    c = cells.shape[0]
    high = cells.astype(jnp.bfloat16)
    split[q, pl.ds(0, c)] = high
    split[q, pl.ds(c, c)] = (cells - high.astype(jnp.float32)).astype(jnp.bfloat16)


def store_halo(split, near, near_at, far, far_at, kept, wide, band):
    odd = lax.rem(lax.axis_index("lat"), 2)
    groups = split.shape[1] // 2 // GROUP
    low_base = REACH + band

    def one(i, _):
        store_split(split, i + low_base * (1 - odd), unpack_rows(near, near_at + (i,), groups, kept, wide))
        store_split(split, i + low_base * odd, unpack_rows(far, far_at + (i,), groups, kept, wide))
        return 0

    lax.fori_loop(0, REACH, one, 0)


def convolve(row_taps, weights, split, stack, r, lags):
    c = split.shape[1] // 2
    taps = row_taps.shape[1]
    for t in range(taps):
        q = row_taps[r, t]
        high = split[q, pl.ds(0, c)]
        stack[pl.ds(2 * t * c, c)] = high
        stack[pl.ds((2 * t + 1) * c, c)] = high
        stack[pl.ds((2 * taps + t) * c, c)] = split[q, pl.ds(c, c)]
    products = jnp.dot(weights[r], stack[...], preferred_element_type=jnp.float32)
    mixed = products[0:c]
    for d in range(1, lags):
        mixed = mixed + shift_left(products[d * c : (d + 1) * c], d)
    return mixed


def clear_tail(stack, taps, c):
    if stack.shape[0] > 3 * taps * c:
        rest = stack.shape[0] - 3 * taps * c
        stack[pl.ds(3 * taps * c, rest)] = jnp.zeros((rest, stack.shape[1]), stack.dtype)


def own_kernel(sizes, row_taps, weights, own_w, near, far, x_own, split, stack):
    band, lags, w, reach2, wide = sizes
    kept = w + 2 * reach2
    clear_tail(stack, row_taps.shape[1], own_w.shape[1])
    store_halo(split, near, (), far, (), kept, wide, band)

    def own(r, _):
        store_split(split, REACH + r, own_w[r])
        return 0

    lax.fori_loop(0, band, own, 0)

    def one_row(r, _):
        mixed = convolve(row_taps, weights, split, stack, r, lags)
        x_own[r] = shift_left(own_w[r], reach2) + gelu(mixed)
        return 0

    lax.fori_loop(0, band, one_row, 0)


def score_kernel(
    sizes, row_taps, area, weights, x_own, oth, near, far, target, g_own, g_oth, loss, split, stack, states
):
    band, n, lags, w, reach2, wide = sizes
    kept = w + 2 * reach2
    c = x_own.shape[1]
    groups = c // GROUP
    clear_tail(stack, row_taps.shape[1], c)
    for step in range(n - 1):
        store_halo(split, near, (step,), far, (step,), kept, wide, band)

        def own(r, _):
            cells = unpack_rows(oth, (step, r), groups, kept, wide)
            store_split(split, REACH + r, cells)
            states[step, r] = shift_left(cells, reach2)
            return 0

        lax.fori_loop(0, band, own, 0)

        def one_row(r, _):
            mixed = convolve(row_taps, weights, split, stack, r, lags)
            states[step, r] = states[step, r] + gelu(mixed)
            return 0

        lax.fori_loop(0, band, one_row, 0)

    def score(r, total):
        weight = area[r]
        truth = target[r]
        xs = [x_own[r]] + [states[step, r] for step in range(n - 1)]
        mean = 1.0 / c
        cell = None
        grads = []
        for x in xs:
            gap = x - truth
            skill = jnp.sqrt(jnp.sum(gap * gap, axis=0, keepdims=True) * mean + 1.0)
            grads.append(gap * (weight / skill))
            cell = skill if cell is None else cell + skill
        cell = cell / n
        for a in range(n):
            for b in range(a + 1, n):
                gap = xs[a] - xs[b]
                distance = jnp.sqrt(jnp.sum(gap * gap, axis=0, keepdims=True) * mean + 1.0)
                pull = gap * (weight / (n * distance))
                grads[a] = grads[a] - pull
                grads[b] = grads[b] + pull
                cell = cell - distance / (n * n)
        cell = cell - 1.0 / (2.0 * n)
        g_own[r] = grads[0]
        for step in range(n - 1):
            pack_rows(g_oth, (step, r), grads[step + 1], w)
        return total + weight * cell

    total = lax.fori_loop(0, band, score, jnp.zeros((1, wide), jnp.float32))
    lane = lax.broadcasted_iota(jnp.int32, (1, wide), 1)
    total = jnp.sum(jnp.where(lane < w, total, 0.0), axis=1, keepdims=True)
    loss[...] = jnp.broadcast_to(total, loss.shape)


def assemble_kernel(sizes, g_own, back, out):
    band, n, w, wide = sizes
    ens = lax.axis_index("ens")
    groups = g_own.shape[1] // GROUP
    total = out.shape[3]
    lane = lax.broadcasted_iota(jnp.int32, (g_own.shape[1], total), 1)
    span = max(total, wide)

    def one_row(r, _):
        result = None
        for step in range(n):
            if step == 0:
                cells = g_own[r]
            else:
                cells = unpack_rows(back, (step - 1, r), groups, w, wide)
            cells = jnp.concatenate([cells, jnp.zeros((cells.shape[0], span - wide), cells.dtype)], axis=1)
            owner = lax.rem(ens + step, n)
            cells = pltpu.roll(cells, owner * w, axis=1)
            mine = jnp.logical_and(lane >= owner * w, lane < (owner + 1) * w)
            result = jnp.where(mine, cells, 0.0) if result is None else jnp.where(mine, cells, result)
        out[r, 0] = result
        return 0

    lax.fori_loop(0, band, one_row, 0)


def shift_pairs(sizes, step):
    n, bands = sizes
    return [(e * bands + l, (e + step) % n * bands + l) for e in range(n) for l in range(bands)]


def halo_pairs(sizes, step, near):
    n, bands = sizes
    starts = range(0, bands - 1, 2) if near else range(1, bands - 1, 2)
    lat = [pair for i in starts for pair in ((i, i + 1), (i + 1, i))]
    return [(e * bands + a, (e + step) % n * bands + b) for e in range(n) for a, b in lat]


def per_device(members, truth, target_time, row_taps, filters, mixing):
    f32 = jnp.float32
    axes = ("ens", "lat")
    n, bands = lax.axis_size("ens"), lax.axis_size("lat")
    sizes = (n, bands)
    band, _, c, total = members.shape
    taps, kinds, lags = filters.shape[2:]
    reach2 = lags // 2
    w = total // n
    kept = w + 2 * reach2
    wide = round_up(kept, LANES)
    packed = round_up(c // GROUP * kept, LANES)
    packed_back = round_up(c // GROUP * w, LANES)
    deep = round_up(3 * taps, 4) * c
    first_row = lax.axis_index("lat") * band
    total_rows = band * bands
    ext = band + 2 * REACH

    def params(mib):
        return pltpu.CompilerParams(vmem_limit_bytes=mib * MIB)

    row = (GROUP, packed)
    own_w, near_own, far_own, oth, far_oth = pl.pallas_call(
        functools.partial(prepare_kernel, (band, n, w, reach2, wide)),
        name="prepare",
        in_specs=[VMEM],
        out_specs=[VMEM] * 5,
        out_shape=[
            jax.ShapeDtypeStruct((band, c, wide), f32),
            jax.ShapeDtypeStruct((REACH,) + row, f32),
            jax.ShapeDtypeStruct((REACH,) + row, f32),
            jax.ShapeDtypeStruct((n - 1, band) + row, f32),
            jax.ShapeDtypeStruct((n - 1, REACH) + row, f32),
        ],
        compiler_params=params(16),
    )(members)

    def along_ens(stack, sign):
        return jnp.stack(
            [lax.ppermute(stack[s - 1], axes, shift_pairs(sizes, sign * s)) for s in range(1, n)]
        )

    def halo_oth(stack, near):
        return jnp.stack(
            [lax.ppermute(stack[s - 1], axes, halo_pairs(sizes, 0 if near else s, near)) for s in range(1, n)]
        )

    oth = along_ens(oth, 1)
    far_oth = halo_oth(far_oth, False)
    far_own = lax.ppermute(far_own, axes, halo_pairs(sizes, 0, False))
    near_own = lax.ppermute(near_own, axes, halo_pairs(sizes, 0, True))

    mix = jnp.transpose(mixing[0], (1, 0, 2))
    mix = jnp.concatenate([mix, mix], axis=2)
    flat = filters[0].reshape(band * taps, kinds * lags)
    weights, target = pl.pallas_call(
        functools.partial(weights_kernel, (band, taps, lags, kinds, w, wide)),
        name="weights",
        in_specs=[SMEM, SMEM, VMEM, ANY],
        out_specs=[VMEM] * 2,
        out_shape=[
            jax.ShapeDtypeStruct((band, lags * c, deep), jnp.bfloat16),
            jax.ShapeDtypeStruct((band, c, wide), f32),
        ],
        scratch_shapes=[pltpu.VMEM((band, c, total), f32), pltpu.SemaphoreType.DMA((band,))],
        compiler_params=params(16),
    )(target_time, flat, mix, truth)

    local_taps = jnp.clip(row_taps[0] - (first_row - REACH), 0, ext - 1)
    scratch = [pltpu.VMEM((ext, 2 * c, wide), jnp.bfloat16), pltpu.VMEM((deep, wide), jnp.bfloat16)]

    odd = lax.rem(lax.axis_index("lat"), 2)
    near_oth = halo_oth(lax.dynamic_slice_in_dim(oth, 1 - odd, REACH, axis=1), True)

    x_own = pl.pallas_call(
        functools.partial(own_kernel, (band, lags, w, reach2, wide)),
        name="convolve_own",
        in_specs=[SMEM] + [VMEM] * 4,
        out_specs=VMEM,
        out_shape=jax.ShapeDtypeStruct((band, c, wide), f32),
        scratch_shapes=scratch,
        compiler_params=params(24),
    )(local_taps, weights, own_w, near_own, far_own)

    latitude = (np.arange(total_rows) + 0.5) * (math.pi / total_rows) - 0.5 * math.pi
    cosine = np.cos(latitude)
    area = lax.dynamic_slice_in_dim(jnp.asarray(cosine / cosine.mean(), f32), first_row, band)

    g_own, g_oth, loss = pl.pallas_call(
        functools.partial(score_kernel, (band, n, lags, w, reach2, wide)),
        name="score",
        in_specs=[SMEM, SMEM] + [VMEM] * 6,
        out_specs=[VMEM] * 3,
        out_shape=[
            jax.ShapeDtypeStruct((band, c, wide), f32),
            jax.ShapeDtypeStruct((n - 1, band, GROUP, packed_back), f32),
            jax.ShapeDtypeStruct((GROUP, LANES), f32),
        ],
        scratch_shapes=scratch + [pltpu.VMEM((n - 1, band, c, wide), f32)],
        compiler_params=params(24),
    )(local_taps, area, weights, x_own, oth, near_oth, far_oth, target)

    back = along_ens(g_oth, -1)
    parts = lax.all_to_all(jnp.full((n * bands,), loss[0, 0]), axes, 0, 0, tiled=True)
    loss_value = jnp.sum(parts).reshape(1) / (total_rows * total)

    score_grad = pl.pallas_call(
        functools.partial(assemble_kernel, (band, n, w, wide)),
        name="assemble",
        in_specs=[VMEM] * 2,
        out_specs=VMEM,
        out_shape=jax.ShapeDtypeStruct(members.shape, f32),
        compiler_params=params(16),
    )(g_own, back)
    return (score_grad, loss_value)


def solution(mesh):
    placed = (
        P("lat", "ens", None, None),
        P(None, "lat", None, None),
        P("lat"),
        P(None, "lat", None),
        P(None, "lat", None, None, None),
        P(),
    )
    return jax.shard_map(
        per_device,
        mesh=mesh,
        in_specs=placed,
        out_specs=(P("lat", "ens", None, None), P()),
        check_vma=False,
    )
```

```python
import functools
import math

import jax
import jax.numpy as jnp
import numpy as np
from jax import lax
from jax.experimental import pallas as pl
from jax.experimental.pallas import tpu as pltpu
from jax.sharding import PartitionSpec as P


REACH = 4
LANES = 128
GROUP = 8
MIB = 1 << 20

VMEM = pl.BlockSpec(memory_space=pltpu.VMEM)
SMEM = pl.BlockSpec(memory_space=pltpu.SMEM)
HBM = pl.BlockSpec(memory_space=pltpu.MemorySpace.HBM)


def round_up(value, unit):
    return -(-value // unit) * unit


def shift_left(cells, amount):
    width = cells.shape[-1]
    amount %= width
    return cells if amount == 0 else pltpu.roll(cells, width - amount, axis=cells.ndim - 1)


def pack_tiles(cells, width, start=0):
    groups = cells.shape[0] // GROUP
    lane = lax.broadcasted_iota(jnp.int32, (GROUP, LANES), 1)
    tiles = []
    for group in range(groups):
        part = cells[group * GROUP : (group + 1) * GROUP]
        offset = group * width % LANES
        count = -(-(offset + width) // LANES)
        pad = count * LANES - part.shape[1]
        if pad > 0:
            part = jnp.concatenate([part, jnp.zeros((GROUP, pad), part.dtype)], axis=1)
        part = shift_left(part, start - offset)
        values = [part[:, i * LANES : (i + 1) * LANES] for i in range(count)]
        if offset:
            values[0] = jnp.where(lane < offset, tiles.pop(), values[0])
        tiles += values
    return tiles


def store_tiles(ref, at, tiles):
    for i, tile in enumerate(tiles):
        ref[at + (slice(None), pl.ds(i * LANES, LANES))] = tile


def unpack_rows(ref, at, groups, width, wide):
    parts = []
    limit = ref.shape[-1]
    for group in range(groups):
        first = group * width
        offset = first % LANES
        base = first - offset
        take = min(wide + (LANES if offset else 0), limit - base)
        part = ref[at + (slice(None), pl.ds(base, take))]
        if take < wide:
            part = jnp.concatenate([part, jnp.zeros((GROUP, wide - take), part.dtype)], axis=1)
        if offset:
            part = shift_left(part, offset)
        parts.append(part[:, :wide])
    return jnp.concatenate(parts, axis=0)


def gelu(v):
    return 0.5 * v * (1.0 + jnp.tanh(math.sqrt(2.0 / math.pi) * (v + 0.044715 * (v * v * v))))


def prepare_kernel(sizes, members, own_w, near_own, far_own, oth, far_oth):
    band, n, w, reach2, wide = sizes
    ens = lax.axis_index("ens")
    odd = lax.rem(lax.axis_index("lat"), 2)
    kept = w + 2 * reach2
    near_from, far_from = 1 - odd, odd
    for p in range(n):
        start = p * w - reach2

        @pl.when(ens != p)
        def _():
            step = lax.rem(p - ens + n, n) - 1
            for r in range(band):
                tiles = pack_tiles(members[r, 0], kept, start)
                store_tiles(oth, (step, r), tiles)
                far_at = r - far_from

                @pl.when(jnp.logical_and(far_at >= 0, far_at < REACH))
                def _():
                    store_tiles(far_oth, (step, far_at), tiles)

        @pl.when(ens == p)
        def _():
            for r in range(band):
                row = members[r, 0]
                own_w[r] = shift_left(row, start)[:, :wide]
                tiles = pack_tiles(row, kept, start)
                near_at, far_at = r - near_from, r - far_from

                @pl.when(jnp.logical_and(near_at >= 0, near_at < REACH))
                def _():
                    store_tiles(near_own, (near_at,), tiles)

                @pl.when(jnp.logical_and(far_at >= 0, far_at < REACH))
                def _():
                    store_tiles(far_own, (far_at,), tiles)


def weights_kernel(sizes, times, filters, mix, truth, weights, target, twice, held, sems):
    band, n, taps, lags, kinds, w, wide = sizes
    copies = [pltpu.make_async_copy(truth.at[times[r], r], held.at[r], sems.at[r]) for r in range(band)]
    for copy in copies:
        copy.start()
    c = mix.shape[1]
    half = lax.broadcasted_iota(jnp.int32, (c, 2 * c), 1) < c
    for k in range(kinds):
        twice[k] = jnp.concatenate([mix[k], mix[k]], axis=1)

    def one_row(r, _):
        for d in range(lags):
            for t in range(0, taps, 2):
                acc = None
                for k in range(kinds):
                    scale = filters[r, t, d, 0, k]
                    if t + 1 < taps:
                        scale = jnp.where(half[:GROUP], scale, filters[r, t + 1, d, 0, k])
                        scale = jnp.concatenate([scale] * (c // GROUP), axis=0)
                    term = scale * twice[k]
                    acc = term if acc is None else acc + term
                high = acc.astype(jnp.bfloat16).astype(jnp.float32)
                low = acc - high
                if t + 1 < taps:
                    blocks = [high, low, high]
                else:
                    blocks = [jnp.where(half, high, low), jnp.where(half, high, 0.0)]
                for i, block in enumerate(blocks):
                    at = (3 * (t // 2) + i) * 2 * c
                    weights[r, pl.ds(d * c, c), pl.ds(at, 2 * c)] = block.astype(jnp.bfloat16)
        return 0

    lax.fori_loop(0, band, one_row, 0)
    ens = lax.axis_index("ens")
    for copy in copies:
        copy.wait()
    for p in range(n):

        @pl.when(ens == p)
        def _():
            for r in range(band):
                target[r] = shift_left(held[r], p * w)[:, :wide]


def store_split(split, q, cells):
    c = cells.shape[0]
    high = cells.astype(jnp.bfloat16)
    split[q, pl.ds(0, c)] = high
    split[q, pl.ds(c, c)] = (cells - high.astype(jnp.float32)).astype(jnp.bfloat16)


def store_halo(split, near, near_at, far, far_at, kept, wide, band):
    odd = lax.rem(lax.axis_index("lat"), 2)
    groups = split.shape[-2] // 2 // GROUP
    low_base = REACH + band
    for ref, at, base in ((near, near_at, low_base * (1 - odd)), (far, far_at, low_base * odd)):
        if ref is not None:
            for i in range(REACH):
                store_split(split, i + base, unpack_rows(ref, at + (i,), groups, kept, wide))


def tap_rows(row_taps, r, band, ext):
    first = lax.axis_index("lat") * band - REACH
    return [
        jnp.clip(row_taps[r, 0, t] - first, 0, ext - 1) for t in range(row_taps.shape[2])
    ]


def convolve(row_taps, weights, split, r, lags, band):
    c = split.shape[1] // 2
    rows = tap_rows(row_taps, r, band, split.shape[0])
    blocks = []
    for t in range(0, len(rows), 2):
        pair = rows[t : t + 2]
        high = [split[q, pl.ds(0, c)] for q in pair]
        low = [split[q, pl.ds(c, c)] for q in pair]
        blocks += high + high + low
        if len(pair) == 1:
            blocks.append(jnp.zeros_like(low[0]))
    stack = jnp.concatenate(blocks, axis=0)
    products = jnp.dot(weights[r], stack, preferred_element_type=jnp.float32)
    mixed = products[0:c]
    for d in range(1, lags):
        mixed = mixed + shift_left(products[d * c : (d + 1) * c], d)
    return mixed


def own_kernel(sizes, row_taps, weights, own_w, near, far, x_own, split):
    band, lags, w, reach2, wide = sizes
    kept = w + 2 * reach2
    store_halo(split, near, (), far, (), kept, wide, band)
    for r in range(band):
        store_split(split, REACH + r, own_w[r])
    for r in range(band):
        mixed = convolve(row_taps, weights, split, r, lags, band)
        x_own[r] = shift_left(own_w[r], reach2) + gelu(mixed)


def receive_kernel(sizes, oth, near, states, split):
    band, n, w, reach2, wide = sizes
    first = 1 - lax.rem(lax.axis_index("lat"), 2)
    for step in range(n - 1):
        for i in range(REACH):
            near[step, i] = oth[step, first + i]
    kept = w + 2 * reach2
    groups = states.shape[2] // GROUP
    for step in range(n - 1):
        for r in range(band):
            cells = unpack_rows(oth, (step, r), groups, kept, wide)
            store_split(split.at[step], REACH + r, cells)
            states[step, r] = shift_left(cells, reach2)


def score_kernel(
    sizes, row_taps, area, weights, x_own, states, near, far, target, split_in, g_own, g_oth, parts, split
):
    band, n, lags, w, reach2, wide = sizes
    kept = w + 2 * reach2
    c = x_own.shape[1]
    first_row = lax.axis_index("lat") * band
    for step in range(n - 1):
        store_halo(split.at[step], near, (step,), far, (step,), kept, wide, band)

    def other_state(step, r):
        return states[step, r] + gelu(convolve(row_taps, weights, split.at[step], r, lags, band))

    def score(r, total):
        weight = area[first_row + r]
        truth = target[r]
        xs = [x_own[r]] + [other_state(step, r) for step in range(n - 1)]
        mean = 1.0 / c
        cell = None
        grads = []
        for x in xs:
            gap = x - truth
            skill = jnp.sqrt(jnp.sum(gap * gap, axis=0, keepdims=True) * mean + 1.0)
            grads.append(gap * (weight / skill))
            cell = skill if cell is None else cell + skill
        cell = cell / n
        for a in range(n):
            for b in range(a + 1, n):
                gap = xs[a] - xs[b]
                distance = jnp.sqrt(jnp.sum(gap * gap, axis=0, keepdims=True) * mean + 1.0)
                pull = gap * (weight / (n * distance))
                grads[a] = grads[a] - pull
                grads[b] = grads[b] + pull
                cell = cell - distance / (n * n)
        cell = cell - 1.0 / (2.0 * n)
        g_own[r] = grads[0]
        for step in range(n - 1):
            store_tiles(g_oth, (step, r), pack_tiles(grads[step + 1], w))
        return total + weight * cell

    total = jnp.zeros((1, wide), jnp.float32)
    for r in range(band):
        total = score(r, total)
    lane = lax.broadcasted_iota(jnp.int32, (1, wide), 1)
    total = jnp.sum(jnp.where(lane < w, total, 0.0), axis=1, keepdims=True)
    parts[...] = jnp.broadcast_to(total[None], parts.shape)


def assemble_kernel(sizes, g_own, back, parts, out, loss):
    band, n, w, wide = sizes
    ens = lax.axis_index("ens")
    groups = g_own.shape[1] // GROUP
    total = out.shape[3]
    lane = lax.broadcasted_iota(jnp.int32, (g_own.shape[1], total), 1)
    span = max(total, wide)

    def one_row(r, _):
        result = None
        for step in range(n):
            if step == 0:
                cells = g_own[r]
            else:
                cells = unpack_rows(back, (step - 1, r), groups, w, wide)
            cells = jnp.concatenate([cells, jnp.zeros((cells.shape[0], span - wide), cells.dtype)], axis=1)
            owner = lax.rem(ens + step, n)
            cells = pltpu.roll(cells, owner * w, axis=1)
            mine = jnp.logical_and(lane >= owner * w, lane < (owner + 1) * w)
            result = jnp.where(mine, cells, 0.0) if result is None else jnp.where(mine, cells, result)
        out[r, 0] = result
        return 0

    lax.fori_loop(0, band, one_row, 0)
    cells = band * (parts.shape[0] // n) * total
    loss[0] = jnp.sum(jnp.sum(parts[...], axis=0)[:, :1]) / cells


def shift_pairs(sizes, step):
    n, bands = sizes
    return [(e * bands + l, (e + step) % n * bands + l) for e in range(n) for l in range(bands)]


def halo_pairs(sizes, step, near):
    n, bands = sizes
    starts = range(0, bands - 1, 2) if near else range(1, bands - 1, 2)
    lat = [pair for i in starts for pair in ((i, i + 1), (i + 1, i))]
    return [(e * bands + a, (e + step) % n * bands + b) for e in range(n) for a, b in lat]


def per_device(members, truth, target_time, row_taps, filters, mixing):
    f32 = jnp.float32
    axes = ("ens", "lat")
    n, bands = lax.axis_size("ens"), lax.axis_size("lat")
    sizes = (n, bands)
    band, _, c, total = members.shape
    taps, kinds, lags = filters.shape[2:]
    reach2 = lags // 2
    row_taps = jnp.transpose(row_taps, (1, 0, 2))
    filters = jnp.transpose(filters, (1, 2, 4, 0, 3))
    mix = jnp.transpose(mixing[0], (1, 0, 2))
    w = total // n
    kept = w + 2 * reach2
    wide = round_up(kept, LANES)
    packed = round_up(c // GROUP * kept, LANES)
    packed_back = round_up(c // GROUP * w, LANES)
    deep = (3 * (taps // 2) + 2 * (taps % 2)) * 2 * c
    total_rows = band * bands
    ext = band + 2 * REACH

    def params(mib):
        return pltpu.CompilerParams(vmem_limit_bytes=mib * MIB)

    def takes(micros):
        return pl.CostEstimate(flops=0, bytes_accessed=int(micros * 3.69e6), transcendentals=0)

    row = (GROUP, packed)
    own_w, near_own, far_own, oth, far_oth = pl.pallas_call(
        functools.partial(prepare_kernel, (band, n, w, reach2, wide)),
        name="prepare",
        cost_estimate=takes(1.2),
        in_specs=[VMEM],
        out_specs=[VMEM] * 5,
        out_shape=[
            jax.ShapeDtypeStruct((band, c, wide), f32),
            jax.ShapeDtypeStruct((REACH,) + row, f32),
            jax.ShapeDtypeStruct((REACH,) + row, f32),
            jax.ShapeDtypeStruct((n - 1, band) + row, f32),
            jax.ShapeDtypeStruct((n - 1, REACH) + row, f32),
        ],
        compiler_params=params(16),
    )(members)

    def along_ens(stack, sign):
        return jnp.stack(
            [lax.ppermute(stack[s - 1], axes, shift_pairs(sizes, sign * s)) for s in range(1, n)]
        )

    def halo_oth(stack, near):
        return jnp.stack(
            [lax.ppermute(stack[s - 1], axes, halo_pairs(sizes, 0 if near else s, near)) for s in range(1, n)]
        )

    oth = along_ens(oth, 1)
    far_own = lax.ppermute(far_own, axes, halo_pairs(sizes, 0, False))
    near_own = lax.ppermute(near_own, axes, halo_pairs(sizes, 0, True))
    far_oth = halo_oth(far_oth, False)

    weights, target = pl.pallas_call(
        functools.partial(weights_kernel, (band, n, taps, lags, kinds, w, wide)),
        name="weights",
        cost_estimate=takes(4.0),
        in_specs=[SMEM, SMEM, VMEM, HBM],
        out_specs=[VMEM] * 2,
        out_shape=[
            jax.ShapeDtypeStruct((band, lags * c, deep), jnp.bfloat16),
            jax.ShapeDtypeStruct((band, c, wide), f32),
        ],
        scratch_shapes=[
            pltpu.VMEM((kinds, c, 2 * c), f32),
            pltpu.VMEM((band, c, total), f32),
            pltpu.SemaphoreType.DMA((band,)),
        ],
        compiler_params=params(47),
    )(target_time, filters, mix, truth)

    split_shape = jax.ShapeDtypeStruct((n - 1, ext, 2 * c, wide), jnp.bfloat16)

    split_shape = jax.ShapeDtypeStruct((n - 1, ext, 2 * c, wide), jnp.bfloat16)

    split_shape = jax.ShapeDtypeStruct((n - 1, ext, 2 * c, wide), jnp.bfloat16)

    split_shape = jax.ShapeDtypeStruct((n - 1, ext, 2 * c, wide), jnp.bfloat16)

    x_own = pl.pallas_call(
        functools.partial(own_kernel, (band, lags, w, reach2, wide)),
        name="convolve_own",
        cost_estimate=takes(3.0),
        in_specs=[SMEM] + [VMEM] * 4,
        out_specs=VMEM,
        out_shape=jax.ShapeDtypeStruct((band, c, wide), f32),
        scratch_shapes=[pltpu.VMEM((ext, 2 * c, wide), jnp.bfloat16)],
        compiler_params=params(24),
    )(row_taps, weights, own_w, near_own, far_own)

    near_oth, states, split_oth = pl.pallas_call(
        functools.partial(receive_kernel, (band, n, w, reach2, wide)),
        name="receive",
        cost_estimate=takes(0.6),
        in_specs=[VMEM],
        out_specs=[VMEM] * 3,
        out_shape=[
            jax.ShapeDtypeStruct((n - 1, REACH) + row, f32),
            jax.ShapeDtypeStruct((n - 1, band, c, wide), f32),
            split_shape,
        ],
        compiler_params=params(24),
    )(oth)
    near_oth = halo_oth(near_oth, True)

    latitude = (np.arange(total_rows) + 0.5) * (math.pi / total_rows) - 0.5 * math.pi
    cosine = np.cos(latitude)
    area = jnp.asarray(cosine / cosine.mean(), f32)

    g_own, g_oth, parts, _ = pl.pallas_call(
        functools.partial(score_kernel, (band, n, lags, w, reach2, wide)),
        name="score",
        cost_estimate=takes(3.1),
        in_specs=[SMEM, SMEM] + [VMEM] * 7,
        out_specs=[VMEM] * 4,
        out_shape=[
            jax.ShapeDtypeStruct((band, c, wide), f32),
            jax.ShapeDtypeStruct((n - 1, band, GROUP, packed_back), f32),
            jax.ShapeDtypeStruct((n * bands, 1, LANES), f32),
            split_shape,
        ],
        input_output_aliases={8: 3},
        compiler_params=params(24),
    )(row_taps, area, weights, x_own, states, near_oth, far_oth, target, split_oth)

    back = along_ens(g_oth, -1)
    parts = lax.all_to_all(parts, axes, 0, 0, tiled=True)

    score_grad, loss_value = pl.pallas_call(
        functools.partial(assemble_kernel, (band, n, w, wide)),
        name="assemble",
        cost_estimate=takes(1.8),
        in_specs=[VMEM] * 3,
        out_specs=[VMEM, SMEM],
        out_shape=[jax.ShapeDtypeStruct(members.shape, f32), jax.ShapeDtypeStruct((1,), f32)],
        compiler_params=params(16),
    )(g_own, back, parts)
    return (score_grad, loss_value)


def solution(mesh):
    placed = (
        P("lat", "ens", None, None),
        P(None, "lat", None, None),
        P("lat"),
        P(None, "lat", None),
        P(None, "lat", None, None, None),
        P(),
    )
    return jax.shard_map(
        per_device,
        mesh=mesh,
        in_specs=placed,
        out_specs=(P("lat", "ens", None, None), P()),
        check_vma=False,
    )
```

```python
import functools
import math

import jax
import jax.numpy as jnp
import numpy as np
from jax import lax
from jax.experimental import pallas as pl
from jax.experimental.pallas import tpu as pltpu
from jax.sharding import PartitionSpec as P


REACH = 4
LANES = 128
GROUP = 8
MIB = 1 << 20

VMEM = pl.BlockSpec(memory_space=pltpu.VMEM)
SMEM = pl.BlockSpec(memory_space=pltpu.SMEM)
HBM = pl.BlockSpec(memory_space=pltpu.MemorySpace.HBM)


def round_up(value, unit):
    return -(-value // unit) * unit


def shift_left(cells, amount):
    width = cells.shape[-1]
    amount %= width
    return cells if amount == 0 else pltpu.roll(cells, width - amount, axis=cells.ndim - 1)


def pack_tiles(cells, width, start=0):
    groups = cells.shape[0] // GROUP
    lane = lax.broadcasted_iota(jnp.int32, (GROUP, LANES), 1)
    tiles = []
    for group in range(groups):
        part = cells[group * GROUP : (group + 1) * GROUP]
        offset = group * width % LANES
        count = -(-(offset + width) // LANES)
        pad = count * LANES - part.shape[1]
        if pad > 0:
            part = jnp.concatenate([part, jnp.zeros((GROUP, pad), part.dtype)], axis=1)
        part = shift_left(part, start - offset)
        values = [part[:, i * LANES : (i + 1) * LANES] for i in range(count)]
        if offset:
            values[0] = jnp.where(lane < offset, tiles.pop(), values[0])
        tiles += values
    return tiles


def store_tiles(ref, at, tiles):
    for i, tile in enumerate(tiles):
        ref[at + (slice(None), pl.ds(i * LANES, LANES))] = tile


def unpack_rows(ref, at, groups, width, wide):
    parts = []
    limit = ref.shape[-1]
    for group in range(groups):
        first = group * width
        offset = first % LANES
        base = first - offset
        take = min(wide + (LANES if offset else 0), limit - base)
        part = ref[at + (slice(None), pl.ds(base, take))]
        if take < wide:
            part = jnp.concatenate([part, jnp.zeros((GROUP, wide - take), part.dtype)], axis=1)
        if offset:
            part = shift_left(part, offset)
        parts.append(part[:, :wide])
    return jnp.concatenate(parts, axis=0)


def gelu(v):
    return 0.5 * v * (1.0 + jnp.tanh(math.sqrt(2.0 / math.pi) * (v + 0.044715 * (v * v * v))))


def prepare_kernel(sizes, members, own_w, near_own, far_own, oth, far_oth):
    band, n, w, reach2, wide = sizes
    ens = lax.axis_index("ens")
    odd = lax.rem(lax.axis_index("lat"), 2)
    kept = w + 2 * reach2
    near_from, far_from = 1 - odd, odd
    for p in range(n):
        start = p * w - reach2

        @pl.when(ens != p)
        def _():
            step = lax.rem(p - ens + n, n) - 1
            for r in range(band):
                tiles = pack_tiles(members[r, 0], kept, start)
                store_tiles(oth, (step, r), tiles)
                far_at = r - far_from

                @pl.when(jnp.logical_and(far_at >= 0, far_at < REACH))
                def _():
                    store_tiles(far_oth, (step, far_at), tiles)

        @pl.when(ens == p)
        def _():
            for r in range(band):
                row = members[r, 0]
                own_w[r] = shift_left(row, start)[:, :wide]
                tiles = pack_tiles(row, kept, start)
                near_at, far_at = r - near_from, r - far_from

                @pl.when(jnp.logical_and(near_at >= 0, near_at < REACH))
                def _():
                    store_tiles(near_own, (near_at,), tiles)

                @pl.when(jnp.logical_and(far_at >= 0, far_at < REACH))
                def _():
                    store_tiles(far_own, (far_at,), tiles)


def weights_kernel(sizes, times, filters, mix, truth, weights, target, twice, held, sems):
    band, n, taps, lags, kinds, w, wide = sizes
    copies = [pltpu.make_async_copy(truth.at[times[r], r], held.at[r], sems.at[r]) for r in range(band)]
    for copy in copies:
        copy.start()
    c = mix.shape[1]
    half = lax.broadcasted_iota(jnp.int32, (c, 2 * c), 1) < c
    for k in range(kinds):
        twice[k] = jnp.concatenate([mix[k], mix[k]], axis=1)

    def one_row(r, _):
        for d in range(lags):
            for t in range(0, taps, 2):
                acc = None
                for k in range(kinds):
                    scale = filters[r, t, d, 0, k]
                    if t + 1 < taps:
                        scale = jnp.where(half[:GROUP], scale, filters[r, t + 1, d, 0, k])
                        scale = jnp.concatenate([scale] * (c // GROUP), axis=0)
                    term = scale * twice[k]
                    acc = term if acc is None else acc + term
                high = acc.astype(jnp.bfloat16).astype(jnp.float32)
                low = acc - high
                if t + 1 < taps:
                    blocks = [high, low, high]
                else:
                    blocks = [jnp.where(half, high, low), jnp.where(half, high, 0.0)]
                for i, block in enumerate(blocks):
                    at = (3 * (t // 2) + i) * 2 * c
                    weights[r, pl.ds(d * c, c), pl.ds(at, 2 * c)] = block.astype(jnp.bfloat16)
        return 0

    lax.fori_loop(0, band, one_row, 0)
    ens = lax.axis_index("ens")
    for copy in copies:
        copy.wait()
    for p in range(n):

        @pl.when(ens == p)
        def _():
            for r in range(band):
                target[r] = shift_left(held[r], p * w)[:, :wide]


def store_split(split, q, cells):
    c = cells.shape[0]
    high = cells.astype(jnp.bfloat16)
    split[q, pl.ds(0, c)] = high
    split[q, pl.ds(c, c)] = (cells - high.astype(jnp.float32)).astype(jnp.bfloat16)


def store_halo(split, near, near_at, far, far_at, kept, wide, band):
    odd = lax.rem(lax.axis_index("lat"), 2)
    groups = split.shape[-2] // 2 // GROUP
    low_base = REACH + band
    for ref, at, base in ((near, near_at, low_base * (1 - odd)), (far, far_at, low_base * odd)):
        if ref is not None:
            for i in range(REACH):
                store_split(split, i + base, unpack_rows(ref, at + (i,), groups, kept, wide))


def tap_rows(row_taps, r, band, ext):
    first = lax.axis_index("lat") * band - REACH
    return [
        jnp.clip(row_taps[r, 0, t] - first, 0, ext - 1) for t in range(row_taps.shape[2])
    ]


def convolve(row_taps, weights, split, r, lags, band):
    c = split.shape[1] // 2
    rows = tap_rows(row_taps, r, band, split.shape[0])
    blocks = []
    for t in range(0, len(rows), 2):
        pair = rows[t : t + 2]
        high = [split[q, pl.ds(0, c)] for q in pair]
        low = [split[q, pl.ds(c, c)] for q in pair]
        blocks += high + high + low
        if len(pair) == 1:
            blocks.append(jnp.zeros_like(low[0]))
    stack = jnp.concatenate(blocks, axis=0)
    products = jnp.dot(weights[r], stack, preferred_element_type=jnp.float32)
    mixed = products[0:c]
    for d in range(1, lags):
        mixed = mixed + shift_left(products[d * c : (d + 1) * c], d)
    return mixed


def split_kernel(own_w, split):
    for r in range(own_w.shape[0]):
        store_split(split, REACH + r, own_w[r])


def own_kernel(sizes, row_taps, weights, own_w, near, far, split_in, x_own, split):
    band, lags, w, reach2, wide = sizes
    kept = w + 2 * reach2
    store_halo(split, near, (), far, (), kept, wide, band)
    for r in range(band):
        mixed = convolve(row_taps, weights, split, r, lags, band)
        x_own[r] = shift_left(own_w[r], reach2) + gelu(mixed)


def receive_kernel(sizes, oth, near, states, split):
    band, n, w, reach2, wide = sizes
    first = 1 - lax.rem(lax.axis_index("lat"), 2)
    for step in range(n - 1):
        for i in range(REACH):
            near[step, i] = oth[step, first + i]
    kept = w + 2 * reach2
    groups = states.shape[2] // GROUP
    for step in range(n - 1):
        for r in range(band):
            cells = unpack_rows(oth, (step, r), groups, kept, wide)
            store_split(split.at[step], REACH + r, cells)
            states[step, r] = shift_left(cells, reach2)


def score_kernel(
    sizes, row_taps, area, weights, x_own, states, near, far, target, split_in, g_own, g_oth, parts, split
):
    band, n, lags, w, reach2, wide = sizes
    kept = w + 2 * reach2
    c = x_own.shape[1]
    first_row = lax.axis_index("lat") * band
    for step in range(n - 1):
        store_halo(split.at[step], near, (step,), far, (step,), kept, wide, band)

    def other_state(step, r):
        return states[step, r] + gelu(convolve(row_taps, weights, split.at[step], r, lags, band))

    def score(r, total):
        weight = area[first_row + r]
        truth = target[r]
        xs = [x_own[r]] + [other_state(step, r) for step in range(n - 1)]
        mean = 1.0 / c
        cell = None
        grads = []
        for x in xs:
            gap = x - truth
            skill = jnp.sqrt(jnp.sum(gap * gap, axis=0, keepdims=True) * mean + 1.0)
            grads.append(gap * (weight / skill))
            cell = skill if cell is None else cell + skill
        cell = cell / n
        for a in range(n):
            for b in range(a + 1, n):
                gap = xs[a] - xs[b]
                distance = jnp.sqrt(jnp.sum(gap * gap, axis=0, keepdims=True) * mean + 1.0)
                pull = gap * (weight / (n * distance))
                grads[a] = grads[a] - pull
                grads[b] = grads[b] + pull
                cell = cell - distance / (n * n)
        cell = cell - 1.0 / (2.0 * n)
        g_own[r] = grads[0]
        for step in range(n - 1):
            store_tiles(g_oth, (step, r), pack_tiles(grads[step + 1], w))
        return total + weight * cell

    total = jnp.zeros((1, wide), jnp.float32)
    for r in range(band):
        total = score(r, total)
    lane = lax.broadcasted_iota(jnp.int32, (1, wide), 1)
    total = jnp.sum(jnp.where(lane < w, total, 0.0), axis=1, keepdims=True)
    parts[...] = jnp.broadcast_to(total[None], parts.shape)


def assemble_kernel(sizes, g_own, back, parts, out, loss, held, sems):
    band, n, w, wide = sizes
    ens = lax.axis_index("ens")
    c, total = held.shape[1:]
    lane = lax.broadcasted_iota(jnp.int32, (c, total), 1)
    copies = [pltpu.make_async_copy(held.at[r], out.at[r, 0], sems.at[r]) for r in range(band)]
    for p in range(n):

        @pl.when(ens == p)
        def _():
            for r in range(band):
                result = None
                for owner in range(n):
                    step = (owner - p) % n
                    cells = g_own[r] if step == 0 else unpack_rows(back, (step - 1, r), c // GROUP, w, wide)
                    if wide < total:
                        cells = jnp.concatenate([cells, jnp.zeros((c, total - wide), cells.dtype)], axis=1)
                    cells = shift_left(cells, -owner * w)[:, :total]
                    result = cells if result is None else jnp.where(lane >= owner * w, cells, result)
                held[r] = result
                copies[r].start()

    cells = band * (parts.shape[0] // n) * total
    loss[0] = jnp.sum(jnp.sum(parts[...], axis=0)[:, :1]) / cells
    for copy in copies:
        copy.wait()


def shift_pairs(sizes, step):
    n, bands = sizes
    return [(e * bands + l, (e + step) % n * bands + l) for e in range(n) for l in range(bands)]


def halo_pairs(sizes, step, near):
    n, bands = sizes
    starts = range(0, bands - 1, 2) if near else range(1, bands - 1, 2)
    lat = [pair for i in starts for pair in ((i, i + 1), (i + 1, i))]
    return [(e * bands + a, (e + step) % n * bands + b) for e in range(n) for a, b in lat]


def per_device(members, truth, target_time, row_taps, filters, mixing):
    f32 = jnp.float32
    axes = ("ens", "lat")
    n, bands = lax.axis_size("ens"), lax.axis_size("lat")
    sizes = (n, bands)
    band, _, c, total = members.shape
    taps, kinds, lags = filters.shape[2:]
    reach2 = lags // 2
    row_taps = jnp.transpose(row_taps, (1, 0, 2))
    filters = jnp.transpose(filters, (1, 2, 4, 0, 3))
    mix = jnp.transpose(mixing[0], (1, 0, 2))
    w = total // n
    kept = w + 2 * reach2
    wide = round_up(kept, LANES)
    packed = round_up(c // GROUP * kept, LANES)
    packed_back = round_up(c // GROUP * w, LANES)
    deep = (3 * (taps // 2) + 2 * (taps % 2)) * 2 * c
    total_rows = band * bands
    ext = band + 2 * REACH

    def params(mib):
        return pltpu.CompilerParams(vmem_limit_bytes=mib * MIB)

    def takes(micros):
        return pl.CostEstimate(flops=0, bytes_accessed=int(micros * 3.69e6), transcendentals=0)

    row = (GROUP, packed)
    own_w, near_own, far_own, oth, far_oth = pl.pallas_call(
        functools.partial(prepare_kernel, (band, n, w, reach2, wide)),
        name="prepare",
        cost_estimate=takes(1.2),
        in_specs=[VMEM],
        out_specs=[VMEM] * 5,
        out_shape=[
            jax.ShapeDtypeStruct((band, c, wide), f32),
            jax.ShapeDtypeStruct((REACH,) + row, f32),
            jax.ShapeDtypeStruct((REACH,) + row, f32),
            jax.ShapeDtypeStruct((n - 1, band) + row, f32),
            jax.ShapeDtypeStruct((n - 1, REACH) + row, f32),
        ],
        compiler_params=params(16),
    )(members)

    def along_ens(stack, sign):
        return jnp.stack(
            [lax.ppermute(stack[s - 1], axes, shift_pairs(sizes, sign * s)) for s in range(1, n)]
        )

    def halo_oth(stack, near):
        return jnp.stack(
            [lax.ppermute(stack[s - 1], axes, halo_pairs(sizes, 0 if near else s, near)) for s in range(1, n)]
        )

    oth = along_ens(oth, 1)
    far_own = lax.ppermute(far_own, axes, halo_pairs(sizes, 0, False))
    near_own = lax.ppermute(near_own, axes, halo_pairs(sizes, 0, True))
    far_oth = halo_oth(far_oth, False)

    own_shape = jax.ShapeDtypeStruct((ext, 2 * c, wide), jnp.bfloat16)
    split_own = pl.pallas_call(
        split_kernel,
        name="split_own",
        cost_estimate=takes(2.0),
        in_specs=[VMEM],
        out_specs=VMEM,
        out_shape=own_shape,
        compiler_params=params(16),
    )(own_w)
    filters, mix, target_time, split_own = lax.optimization_barrier((filters, mix, target_time, split_own))

    weights, target = pl.pallas_call(
        functools.partial(weights_kernel, (band, n, taps, lags, kinds, w, wide)),
        name="weights",
        cost_estimate=takes(4.0),
        in_specs=[SMEM, SMEM, VMEM, HBM],
        out_specs=[VMEM] * 2,
        out_shape=[
            jax.ShapeDtypeStruct((band, lags * c, deep), jnp.bfloat16),
            jax.ShapeDtypeStruct((band, c, wide), f32),
        ],
        scratch_shapes=[
            pltpu.VMEM((kinds, c, 2 * c), f32),
            pltpu.VMEM((band, c, total), f32),
            pltpu.SemaphoreType.DMA((band,)),
        ],
        compiler_params=params(47),
    )(target_time, filters, mix, truth)

    split_shape = jax.ShapeDtypeStruct((n - 1, ext, 2 * c, wide), jnp.bfloat16)

    split_shape = jax.ShapeDtypeStruct((n - 1, ext, 2 * c, wide), jnp.bfloat16)

    split_shape = jax.ShapeDtypeStruct((n - 1, ext, 2 * c, wide), jnp.bfloat16)

    split_shape = jax.ShapeDtypeStruct((n - 1, ext, 2 * c, wide), jnp.bfloat16)

    x_own, _ = pl.pallas_call(
        functools.partial(own_kernel, (band, lags, w, reach2, wide)),
        name="convolve_own",
        cost_estimate=takes(3.0),
        in_specs=[SMEM] + [VMEM] * 5,
        out_specs=[VMEM] * 2,
        out_shape=[jax.ShapeDtypeStruct((band, c, wide), f32), own_shape],
        input_output_aliases={5: 1},
        compiler_params=params(24),
    )(row_taps, weights, own_w, near_own, far_own, split_own)

    near_oth, states, split_oth = pl.pallas_call(
        functools.partial(receive_kernel, (band, n, w, reach2, wide)),
        name="receive",
        cost_estimate=takes(0.6),
        in_specs=[VMEM],
        out_specs=[VMEM] * 3,
        out_shape=[
            jax.ShapeDtypeStruct((n - 1, REACH) + row, f32),
            jax.ShapeDtypeStruct((n - 1, band, c, wide), f32),
            split_shape,
        ],
        compiler_params=params(24),
    )(oth)
    near_oth = halo_oth(near_oth, True)

    latitude = (np.arange(total_rows) + 0.5) * (math.pi / total_rows) - 0.5 * math.pi
    cosine = np.cos(latitude)
    area = jnp.asarray(cosine / cosine.mean(), f32)

    g_own, g_oth, parts, _ = pl.pallas_call(
        functools.partial(score_kernel, (band, n, lags, w, reach2, wide)),
        name="score",
        cost_estimate=takes(3.1),
        in_specs=[SMEM, SMEM] + [VMEM] * 7,
        out_specs=[VMEM] * 4,
        out_shape=[
            jax.ShapeDtypeStruct((band, c, wide), f32),
            jax.ShapeDtypeStruct((n - 1, band, GROUP, packed_back), f32),
            jax.ShapeDtypeStruct((n * bands, 1, LANES), f32),
            split_shape,
        ],
        input_output_aliases={8: 3},
        compiler_params=params(24),
    )(row_taps, area, weights, x_own, states, near_oth, far_oth, target, split_oth)

    back = along_ens(g_oth, -1)
    parts = lax.all_to_all(parts, axes, 0, 0, tiled=True)

    score_grad, loss_value = pl.pallas_call(
        functools.partial(assemble_kernel, (band, n, w, wide)),
        name="assemble",
        cost_estimate=takes(1.8),
        in_specs=[VMEM] * 3,
        out_specs=[HBM, SMEM],
        out_shape=[jax.ShapeDtypeStruct(members.shape, f32), jax.ShapeDtypeStruct((1,), f32)],
        scratch_shapes=[pltpu.VMEM((band, c, total), f32), pltpu.SemaphoreType.DMA((band,))],
        compiler_params=params(16),
    )(g_own, back, parts)
    return (score_grad, loss_value)


def solution(mesh):
    placed = (
        P("lat", "ens", None, None),
        P(None, "lat", None, None),
        P("lat"),
        P(None, "lat", None),
        P(None, "lat", None, None, None),
        P(),
    )
    return jax.shard_map(
        per_device,
        mesh=mesh,
        in_specs=placed,
        out_specs=(P("lat", "ens", None, None), P()),
        check_vma=False,
    )
```
